32 devices in a mesh: ga: 2 (over y), ea: 16 (over z, x, core).
Axes of the slice: x: 2, y: 2, z: 4, core: 2. Of those that a mesh axis runs over, the one named last changes fastest.
Arguments:
- tokens: bfloat16 [4096, 2048], P(('ga', 'ea')), parts along dimension 0, may hold values from -6 to 6
- expert_choice_index: int32 [4096, 4], P(('ga', 'ea')), parts along dimension 0, may hold values from 0 to 7, all different within a row; in each aligned block of 128 rows (0 to 127, 128 to 255, ...) at most 72 rows name the same one
- router_gate_weight: float32 [4096, 4], P(('ga', 'ea')), parts along dimension 0, may hold values from 0.05 to 0.6
- cotangent: bfloat16 [4096, 2048], P(('ga', 'ea')), parts along dimension 0, may hold values from -6 to 6
- gate_up_matrix: bfloat16 [16, 2048, 1408], P('ea'), may hold values from -0.125 to 0.125
- down_weight: bfloat16 [16, 704, 2048], P('ea'), may hold values from -0.15625 to 0.15625
- adapter_input_projection: bfloat16 [2048, 16], replicated, may hold values from -0.125 to 0.125
- adapter_output_projection: bfloat16 [16, 16, 1408], P('ea'), may hold values from -0.59765625 to 0.59765625
Outputs:
- layer_output: bfloat16 [4096, 2048], P(('ga', 'ea')), parts along dimension 0
- adapter_input_gradient: float32 [4096, 16], P('ga'), parts along dimension 0
- lora_b_grad: float32 [32, 16, 1408], P(('ga', 'ea')), parts along dimension 0
The draws below stay inside these ranges and needn't reach their ends.
There are 2 independent parts, one for each index of `ga`. The reference program is written for one: setup_inputs(seed, part) draws one part's arguments, and reference() takes and returns one part's arrays. A program takes and returns all parts, laid end to end along the dimension named above; an argument that names none is the same for every part. Nothing has to cross between parts.
Inputs may be any that keep to these rules, and one draw needn't show every extreme that they name: `expert_choice_index`: each row names 4 different experts. Within the rows of one device (aligned blocks of 128 rows) no expert is named by more than 72 rows, and in every draw some expert is named by exactly 72 rows of some block.
All inputs are finite; a program needn't handle non-finite values.
Results may differ from the reference program's by a relative error of at most 0.0072.
Values may be sent and summed in bfloat16 or wider, within the bound.
A program may use at most 128 MiB of HBM per device.

```python
import math
import jax
import jax.numpy as jnp
import numpy as np
from jax import lax

MODEL_DIM = 2048
FF = 1408
TOP = 4
ADAPTER_RANK = 16
EXPERT_SPLIT = 2
TOK_DEV = 128
EXPERT_COUNT = 8
BLOCK_HIDDEN = 704
HIDDEN_BLOCKS = 16
CAP = 72
TOKENS = 2048
N_EA = 16


def levels(rng, dims, split, smallest, top_value):
    level = 1.0
    for axis_at, shards_of in split:
        draws = jax.random.uniform(jax.random.fold_in(jax.random.fold_in(rng, 6), axis_at), (shards_of,), jnp.float32, smallest / len(split), top_value / len(split))
        level = level * jnp.repeat(jnp.exp(draws), dims[axis_at] // shards_of).reshape((-1,) + (1,) * (len(dims) - 1 - axis_at))
    return level


def assign_block(own_key, own, number, rows, number_of, top, reach, slope):
    sequence = jax.random.permutation(own_key, number_of)
    packed, usual = portions_of(number_of, rows * top, reach, slope, True), portions_of(number_of, rows * top, reach, slope, False)
    places = jnp.arange(number_of)

    def named(tallies, turn):
        used = int((tallies > 0).sum())
        fixed = max(1, used // 4)
        moved = fixed + (places - fixed + turn * (used - fixed)) % max(1, number_of - fixed)
        return jnp.zeros((number_of,), jnp.int32).at[sequence[jnp.where(places < fixed, places, moved)]].set(jnp.asarray(tallies, jnp.int32))

    tallies = jnp.where(number % 4 == 0, named(packed, number // 4), named(usual, number - number // 4 - 1))
    mixed = jax.random.permutation(jax.random.fold_in(own, 3), number_of)
    giver, receiver = mixed[0:number_of // 2 * 2:2], mixed[1:number_of // 2 * 2:2]
    margin = jnp.minimum(tallies[giver] - 1, reach - tallies[receiver]) // 2
    margin = jnp.where((giver == sequence[0]) | (receiver == sequence[0]) | (tallies[receiver] == 0), 0, jnp.maximum(margin, 0))
    moved = jax.random.randint(jax.random.fold_in(own, 4), (number_of // 2,), 0, 1 << 20) % (margin + 1)
    tallies = tallies.at[giver].add(-moved).at[receiver].add(moved)
    members = jnp.searchsorted(jnp.cumsum(tallies), jnp.arange(rows * top), side="right").astype(jnp.int32)
    listing = members.reshape(top, rows).T
    listing = listing[jax.random.permutation(jax.random.fold_in(own, 1), rows)]
    turn = jax.random.randint(jax.random.fold_in(own, 2), (rows, 1), 0, top)
    return jnp.take_along_axis(listing, (jnp.arange(top)[None, :] + turn) % top, axis=1)


def portions_of(amount, total, bound, skew, full):
    weights = [(1 << 20) // math.isqrt(rank ** skew) + 1 for rank in range(1, amount + 1)]
    largest = bound if full else min(bound, max(-(-total // amount), total * weights[0] // sum(weights)))
    least = 1 if total - largest >= amount - 1 else 0
    counts, surplus = [largest] + [least] * (amount - 1), total - largest - least * (amount - 1)
    while surplus > 0:
        free = [i for i in range(1, amount) if counts[i] < largest] or [i for i in range(1, amount) if counts[i] < bound]
        mass, left = sum([weights[i] for i in free]), surplus
        for i in free:
            addition = min(bound - counts[i], max(1, left * weights[i] // mass), surplus)
            counts[i] = counts[i] + addition
            surplus = surplus - addition
    return np.array(counts)


def normal_values(own_key, extent, width, most, pieces=(), kind=jnp.bfloat16):
    gain = levels(own_key, extent, pieces, -0.22, 0.18) if pieces else 1.0
    values = jax.random.normal(own_key, extent, jnp.float32) * width * gain
    return jnp.minimum(jnp.maximum(values, -most), most).astype(kind)


def setup_inputs(seed: int = 0, part: int = 0) -> dict:
    key_of = jax.random.split(jax.random.key(seed), 9)
    part_keys = jax.random.split(jax.random.fold_in(key_of[8], part), 9)
    tokens = normal_values(part_keys[0], (TOKENS, MODEL_DIM), 1.0, 6.0, ((0, 16),))
    expert_choice_index_keys = jax.random.split(jax.random.fold_in(part_keys[1], 1), TOKENS // TOK_DEV)
    expert_choice_index_turns = jax.random.permutation(jax.random.fold_in(part_keys[1], 3), TOKENS // TOK_DEV)
    expert_choice_index = jax.vmap(lambda own, number: assign_block(jax.random.fold_in(part_keys[1], 2), own, number, TOK_DEV, EXPERT_COUNT, TOP, CAP, 2))(expert_choice_index_keys, expert_choice_index_turns).reshape((TOKENS, TOP))
    router_gate_weight = jnp.clip(0.05 + 0.55 * jax.random.uniform(part_keys[2], (TOKENS, TOP), jnp.float32) ** levels(part_keys[2], (TOKENS, TOP), ((0, 16),), -0.2, 0.2), 0.05, 0.6)
    cotangent = normal_values(part_keys[3], (TOKENS, MODEL_DIM), 1.0, 6.0, ((0, 16),))
    gate_up_matrix = normal_values(key_of[4], (HIDDEN_BLOCKS, MODEL_DIM, 2 * BLOCK_HIDDEN), MODEL_DIM ** -0.5, 0.125, ((0, 16),))
    down_weight = normal_values(key_of[5], (HIDDEN_BLOCKS, BLOCK_HIDDEN, MODEL_DIM), FF ** -0.5, 0.15625, ((0, 16),))
    adapter_input_projection = normal_values(key_of[6], (MODEL_DIM, ADAPTER_RANK), MODEL_DIM ** -0.5, 0.125)
    adapter_output_projection = normal_values(key_of[7], (HIDDEN_BLOCKS, ADAPTER_RANK, 2 * BLOCK_HIDDEN), 0.1, 0.59765625, ((0, 16),))
    return {"tokens": tokens, "expert_choice_index": expert_choice_index, "router_gate_weight": router_gate_weight, "cotangent": cotangent, "gate_up_matrix": gate_up_matrix, "down_weight": down_weight, "adapter_input_projection": adapter_input_projection, "adapter_output_projection": adapter_output_projection}


adapter_scale = 2.0


def slot_ranks(id_block, experts):
    flat_ids = id_block.reshape(-1)
    onehot = (flat_ids[:, None] == jnp.arange(experts, dtype=jnp.int32)[None, :]).astype(jnp.int32)
    before = jnp.cumsum(onehot, axis=0) - onehot
    return jnp.sum(before * onehot, axis=1).reshape(id_block.shape).astype(jnp.int32)


def block_halfway(input_rows, output_gradient_rows, gate_up_weight, down_w, adapter_a, adapter_output_weight):
    adapter_input_rows = jnp.dot(input_rows, adapter_a, preferred_element_type=jnp.float32).astype(jnp.bfloat16)
    joined_columns = jnp.dot(input_rows, gate_up_weight, preferred_element_type=jnp.float32) + adapter_scale * jnp.dot(adapter_input_rows, adapter_output_weight, preferred_element_type=jnp.float32)
    block_width = down_w.shape[0]
    gate_part = joined_columns[:, :block_width]
    up_part = joined_columns[:, block_width:]
    sigmoid_gate = jax.nn.sigmoid(gate_part)
    active = gate_part * sigmoid_gate
    hidden = (active * up_part).astype(jnp.bfloat16)
    partial_value = jnp.dot(hidden, down_w, preferred_element_type=jnp.float32).astype(jnp.bfloat16)
    down_grad = lax.dot_general(output_gradient_rows, down_w, (((1,), (1,)), ((), ())), preferred_element_type=jnp.float32)
    gate_grad = down_grad * up_part * sigmoid_gate * (1.0 + gate_part * (1.0 - sigmoid_gate))
    up_grad = down_grad * active
    joined_gradient = jnp.concatenate([gate_grad, up_grad], axis=1).astype(jnp.bfloat16)
    output_gradient_part = adapter_scale * lax.dot_general(adapter_input_rows, joined_gradient, (((0,), (0,)), ((), ())), preferred_element_type=jnp.float32)
    adapter_gradient = (adapter_scale * lax.dot_general(joined_gradient, adapter_output_weight, (((1,), (1,)), ((), ())), preferred_element_type=jnp.float32)).astype(jnp.bfloat16)
    grad_a = lax.dot_general(input_rows, adapter_gradient, (((0,), (0,)), ((), ())), preferred_element_type=jnp.float32)
    return partial_value, grad_a, output_gradient_part


def reference(tokens, expert_choice_index, router_gate_weight, cotangent, gate_up_matrix, down_weight, adapter_input_projection, adapter_output_projection):
    def block_rank(id_block):
        return slot_ranks(id_block, EXPERT_COUNT)

    slot_rank = jax.vmap(block_rank)(expert_choice_index.reshape(N_EA, TOK_DEV, TOP)).reshape(TOKENS, TOP)
    source = (jnp.arange(TOKENS, dtype=jnp.int32) // TOK_DEV)[:, None] * jnp.ones((1, TOP), jnp.int32)
    token_index = jnp.arange(TOKENS, dtype=jnp.int32)[:, None] * jnp.ones((1, TOP), jnp.int32)
    slot_token = jnp.zeros((EXPERT_COUNT, N_EA, CAP), jnp.int32).at[expert_choice_index, source, slot_rank].set(token_index)
    slot_weight = jnp.zeros((EXPERT_COUNT, N_EA, CAP), jnp.float32).at[expert_choice_index, source, slot_rank].set(router_gate_weight)
    slot_filled = jnp.zeros((EXPERT_COUNT, N_EA, CAP), jnp.bool_).at[expert_choice_index, source, slot_rank].set(True)
    gate_up_pairs = gate_up_matrix.reshape(EXPERT_COUNT, EXPERT_SPLIT, MODEL_DIM, 2 * BLOCK_HIDDEN)
    down_pairs = down_weight.reshape(EXPERT_COUNT, EXPERT_SPLIT, BLOCK_HIDDEN, MODEL_DIM)
    adapter_couples = adapter_output_projection.reshape(EXPERT_COUNT, EXPERT_SPLIT, ADAPTER_RANK, 2 * BLOCK_HIDDEN)

    def one_expert(carry, inputs):
        out_sum, adapter_sum = carry
        index_rows, weight_rows, filled_rows, gate_up_couple, down_couple, adapter_couple = inputs
        slot_index = index_rows.reshape(-1).astype(jnp.int32)
        slot_prob = weight_rows.reshape(-1)
        filled_flag = filled_rows.reshape(-1)
        input_rows = jnp.where(filled_flag[:, None], tokens[slot_index], jnp.zeros((), jnp.bfloat16))
        output_gradient_rows = (slot_prob[:, None] * cotangent[slot_index].astype(jnp.float32)).astype(jnp.bfloat16)
        lower_block_part = block_halfway(input_rows, output_gradient_rows, gate_up_couple[0], down_couple[0], adapter_input_projection, adapter_couple[0])
        upper_block_part = block_halfway(input_rows, output_gradient_rows, gate_up_couple[1], down_couple[1], adapter_input_projection, adapter_couple[1])
        merged = (lower_block_part[0].astype(jnp.float32) + upper_block_part[0].astype(jnp.float32)).astype(jnp.bfloat16)
        out_sum = out_sum.at[slot_index].add(slot_prob[:, None] * merged.astype(jnp.float32))
        adapter_sum = adapter_sum + lower_block_part[1] + upper_block_part[1]
        return (out_sum, adapter_sum), jnp.stack([lower_block_part[2], upper_block_part[2]])

    start = (jnp.zeros((TOKENS, MODEL_DIM), jnp.float32), jnp.zeros((MODEL_DIM, ADAPTER_RANK), jnp.float32))
    (out_sum, adapter_sum), grads_b = lax.scan(one_expert, start, (slot_token, slot_weight, slot_filled, gate_up_pairs, down_pairs, adapter_couples))
    return out_sum.astype(jnp.bfloat16), adapter_sum, grads_b.reshape(HIDDEN_BLOCKS, ADAPTER_RANK, 2 * BLOCK_HIDDEN)
```

```python
import jax
import jax.numpy as jnp
from jax import lax
from jax.sharding import PartitionSpec as P

EXPERT_SPLIT = 2


adapter_scale = 2.0


def from_partner(value, axis, distance):
    mask = 2**distance
    pairs = [(source, source ^ mask) for source in range(lax.axis_size(axis))]
    return lax.ppermute(value, axis, pairs)


def slot_ranks(id_block, experts):
    flat_ids = id_block.reshape(-1)
    onehot = (flat_ids[:, None] == jnp.arange(experts, dtype=jnp.int32)[None, :]).astype(jnp.int32)
    before = jnp.cumsum(onehot, axis=0) - onehot
    return jnp.sum(before * onehot, axis=1).reshape(id_block.shape)


def block_halfway(
    input_rows, output_gradient_rows, gate_up_weight, down_w, adapter_a, adapter_output_weight
):
    adapter_input_rows = jnp.dot(input_rows, adapter_a, preferred_element_type=jnp.float32).astype(
        jnp.bfloat16
    )
    joined_columns = jnp.dot(
        input_rows, gate_up_weight, preferred_element_type=jnp.float32
    ) + adapter_scale * jnp.dot(
        adapter_input_rows, adapter_output_weight, preferred_element_type=jnp.float32
    )
    block_width = down_w.shape[0]
    gate_part = joined_columns[:, :block_width]
    up_part = joined_columns[:, block_width:]
    sigmoid_gate = jax.nn.sigmoid(gate_part)
    active = gate_part * sigmoid_gate
    hidden = (active * up_part).astype(jnp.bfloat16)
    partial_value = jnp.dot(hidden, down_w, preferred_element_type=jnp.float32).astype(jnp.bfloat16)
    down_grad = lax.dot_general(
        output_gradient_rows, down_w, (((1,), (1,)), ((), ())), preferred_element_type=jnp.float32
    )
    gate_grad = down_grad * up_part * sigmoid_gate * (1.0 + gate_part * (1.0 - sigmoid_gate))
    up_grad = down_grad * active
    joined_gradient = jnp.concatenate([gate_grad, up_grad], axis=1).astype(jnp.bfloat16)
    output_gradient_part = adapter_scale * lax.dot_general(
        adapter_input_rows,
        joined_gradient,
        (((0,), (0,)), ((), ())),
        preferred_element_type=jnp.float32,
    )
    adapter_gradient = (
        adapter_scale
        * lax.dot_general(
            joined_gradient,
            adapter_output_weight,
            (((1,), (1,)), ((), ())),
            preferred_element_type=jnp.float32,
        )
    ).astype(jnp.bfloat16)
    grad_a = lax.dot_general(
        input_rows, adapter_gradient, (((0,), (0,)), ((), ())), preferred_element_type=jnp.float32
    )
    return (partial_value, grad_a, output_gradient_part)


def local(
    tokens,
    expert_choice_index,
    router_gate_weight,
    cotangent,
    gate_up_matrix,
    down_weight,
    adapter_input_projection,
    adapter_output_projection,
):
    devices = lax.axis_size("ea")
    experts = devices // EXPERT_SPLIT
    tok_rows, model_width = tokens.shape
    top_count = expert_choice_index.shape[1]
    capacity = 9 * tok_rows * top_count // (8 * experts)
    half_width = model_width // 2
    parity = lax.axis_index("ea") % 2
    slot_rank = slot_ranks(expert_choice_index, experts)
    slot_rows = (expert_choice_index * capacity + slot_rank).reshape(-1)
    scaled_dy = (router_gate_weight[:, :, None] * cotangent[:, None, :].astype(jnp.float32)).astype(
        jnp.bfloat16
    )
    repeated = jnp.broadcast_to(tokens[:, None, :], (tok_rows, top_count, model_width))
    both_rows = jnp.stack([repeated, scaled_dy], axis=2).reshape(
        tok_rows * top_count, 2, model_width
    )
    blank_rows = jnp.zeros((experts * capacity, 2, model_width), jnp.bfloat16)
    send_rows = blank_rows.at[slot_rows].set(both_rows, unique_indices=True)
    rows_total = devices * capacity
    halves = (
        send_rows.reshape(experts, capacity, 2, 2, half_width)
        .transpose(0, 3, 1, 2, 4)
        .reshape(devices, capacity, 2, half_width)
    )
    own_piece = lax.all_to_all(halves, "ea", split_axis=0, concat_axis=0, tiled=True)
    other_piece = from_partner(own_piece, "ea", 0)
    lower_block_part = jnp.where(parity == 0, own_piece, other_piece)
    upper_block_part = jnp.where(parity == 0, other_piece, own_piece)
    arrived = jnp.concatenate([lower_block_part, upper_block_part], axis=3)
    input_rows = arrived[:, :, 0].reshape(rows_total, model_width)
    output_gradient_rows = arrived[:, :, 1].reshape(rows_total, model_width)
    partial_value, input_gradient_local, output_gradient_part = block_halfway(
        input_rows,
        output_gradient_rows,
        gate_up_matrix[0],
        down_weight[0],
        adapter_input_projection,
        adapter_output_projection[0],
    )
    adapter_input_gradient = lax.psum(input_gradient_local, "ea")
    partial_value = partial_value.reshape(devices, capacity, model_width)
    kept_part = jnp.where(
        parity == 0, partial_value[:, :, :half_width], partial_value[:, :, half_width:]
    )
    given_part = jnp.where(
        parity == 0, partial_value[:, :, half_width:], partial_value[:, :, :half_width]
    )
    taken_part = from_partner(given_part, "ea", 0)
    summed = (kept_part.astype(jnp.float32) + taken_part.astype(jnp.float32)).astype(jnp.bfloat16)
    returned = lax.all_to_all(summed, "ea", split_axis=0, concat_axis=0, tiled=True)
    expert_out = (
        returned.reshape(experts, 2, capacity, half_width)
        .transpose(0, 2, 1, 3)
        .reshape(experts * capacity, model_width)
    )
    picked = expert_out[slot_rows].reshape(tok_rows, top_count, model_width).astype(jnp.float32)
    layer_output = jnp.sum(router_gate_weight[:, :, None] * picked, axis=1).astype(jnp.bfloat16)
    return (layer_output, adapter_input_gradient, output_gradient_part[None])


def shared_local(
    tokens,
    expert_choice_index,
    router_gate_weight,
    cotangent,
    gate_up_matrix,
    down_weight,
    adapter_input_projection,
    adapter_output_projection,
):
    devices = lax.axis_size("ea")
    experts = devices // EXPERT_SPLIT
    tok_rows, model_width = tokens.shape
    top_count = expert_choice_index.shape[1]
    capacity = 9 * tok_rows * top_count // (8 * experts)
    rows_total = devices * capacity
    mine = lax.axis_index("ea") // EXPERT_SPLIT
    block_width = down_weight.shape[1]
    adapter_a = adapter_input_projection
    gate_up_weight, down_w, adapter_out = gate_up_matrix[0], down_weight[0], adapter_output_projection[0]

    choice = lax.all_gather(
        jnp.concatenate([expert_choice_index.astype(jnp.float32), router_gate_weight], axis=1), "ea"
    )
    all_tokens = lax.all_gather(tokens, "ea")
    all_cotangent = lax.all_gather(cotangent, "ea")
    named = choice[:, :, :top_count].astype(jnp.int32) == mine
    weight = jnp.sum(jnp.where(named, choice[:, :, top_count:], 0.0), axis=2)
    chosen = jnp.any(named, axis=2)
    place = jnp.cumsum(chosen.astype(jnp.int32), axis=1) - 1
    place = jnp.where(chosen, place, capacity)
    pick = place[:, None, :] == jnp.arange(capacity, dtype=jnp.int32)[None, :, None]
    select = pick.astype(jnp.bfloat16)
    row_weight = jnp.sum(jnp.where(pick, weight[:, None, :], 0.0), axis=2)

    input_rows = jnp.einsum(
        "sct,std->scd", select, all_tokens, preferred_element_type=jnp.bfloat16
    ).reshape(rows_total, model_width)
    adapter_rows = jnp.dot(input_rows, adapter_a, preferred_element_type=jnp.float32).astype(jnp.bfloat16)
    joined = jnp.dot(
        input_rows, gate_up_weight, preferred_element_type=jnp.float32
    ) + adapter_scale * jnp.dot(adapter_rows, adapter_out, preferred_element_type=jnp.float32)
    gate_part, up_part = joined[:, :block_width], joined[:, block_width:]
    sigmoid_gate = jax.nn.sigmoid(gate_part)
    active = gate_part * sigmoid_gate
    hidden = (active * up_part).astype(jnp.bfloat16)
    partial_value = jnp.dot(hidden, down_w, preferred_element_type=jnp.float32).astype(jnp.bfloat16)
    spread = jnp.einsum(
        "sct,scd->std",
        select,
        partial_value.reshape(devices, capacity, model_width),
        preferred_element_type=jnp.float32,
    )
    term = (weight[:, :, None] * spread).astype(jnp.bfloat16).reshape(devices * tok_rows, model_width)
    layer_output = lax.psum_scatter(term, "ea", scatter_dimension=0, tiled=True)

    gradient_rows = jnp.einsum(
        "sct,std->scd", select, all_cotangent, preferred_element_type=jnp.float32
    )
    gradient_rows = (
        (row_weight[:, :, None] * gradient_rows).astype(jnp.bfloat16).reshape(rows_total, model_width)
    )
    down_grad = lax.dot_general(
        gradient_rows, down_w, (((1,), (1,)), ((), ())), preferred_element_type=jnp.float32
    )
    gate_grad = down_grad * up_part * sigmoid_gate * (1.0 + gate_part * (1.0 - sigmoid_gate))
    up_grad = down_grad * active
    joined_gradient = jnp.concatenate([gate_grad, up_grad], axis=1).astype(jnp.bfloat16)
    lora_b = adapter_scale * lax.dot_general(
        adapter_rows, joined_gradient, (((0,), (0,)), ((), ())), preferred_element_type=jnp.float32
    )
    adapter_gradient = (
        adapter_scale
        * lax.dot_general(
            joined_gradient, adapter_out, (((1,), (1,)), ((), ())), preferred_element_type=jnp.float32
        )
    ).astype(jnp.bfloat16)
    grad_a = lax.dot_general(
        input_rows, adapter_gradient, (((0,), (0,)), ((), ())), preferred_element_type=jnp.float32
    )
    return (layer_output, lax.psum(grad_a, "ea"), lora_b[None])


def solution(mesh):
    in_specs = (
        P(("ga", "ea"), None),
        P(("ga", "ea"), None),
        P(("ga", "ea"), None),
        P(("ga", "ea"), None),
        P("ea", None, None),
        P("ea", None, None),
        P(),
        P("ea", None, None),
    )
    out_specs = (P(("ga", "ea"), None), P("ga", None), P(("ga", "ea"), None, None))
    few = mesh.shape["ea"] // EXPERT_SPLIT

    def chosen(*args):
        wide = few > 2 * args[1].shape[1]
        body = local if wide else shared_local
        return jax.shard_map(
            body, mesh=mesh, in_specs=in_specs, out_specs=out_specs, check_vma=False
        )(*args)

    return chosen
```

```python
import jax
import jax.numpy as jnp
from jax import lax
from jax.sharding import PartitionSpec as P

EXPERT_SPLIT = 2
PLANE = 4


adapter_scale = 2.0


def from_partner(value, axis, distance):
    mask = 2**distance
    pairs = [(source, source ^ mask) for source in range(lax.axis_size(axis))]
    return lax.ppermute(value, axis, pairs)


def slot_ranks(id_block, experts):
    flat_ids = id_block.reshape(-1)
    onehot = (flat_ids[:, None] == jnp.arange(experts, dtype=jnp.int32)[None, :]).astype(jnp.int32)
    before = jnp.cumsum(onehot, axis=0) - onehot
    return jnp.sum(before * onehot, axis=1).reshape(id_block.shape)


def block_halfway(
    input_rows, output_gradient_rows, gate_up_weight, down_w, adapter_a, adapter_output_weight
):
    adapter_input_rows = jnp.dot(input_rows, adapter_a, preferred_element_type=jnp.float32).astype(
        jnp.bfloat16
    )
    joined_columns = jnp.dot(
        input_rows, gate_up_weight, preferred_element_type=jnp.float32
    ) + adapter_scale * jnp.dot(
        adapter_input_rows, adapter_output_weight, preferred_element_type=jnp.float32
    )
    block_width = down_w.shape[0]
    gate_part = joined_columns[:, :block_width]
    up_part = joined_columns[:, block_width:]
    sigmoid_gate = jax.nn.sigmoid(gate_part)
    active = gate_part * sigmoid_gate
    hidden = (active * up_part).astype(jnp.bfloat16)
    partial_value = jnp.dot(hidden, down_w, preferred_element_type=jnp.float32).astype(jnp.bfloat16)
    down_grad = lax.dot_general(
        output_gradient_rows, down_w, (((1,), (1,)), ((), ())), preferred_element_type=jnp.float32
    )
    gate_grad = down_grad * up_part * sigmoid_gate * (1.0 + gate_part * (1.0 - sigmoid_gate))
    up_grad = down_grad * active
    joined_gradient = jnp.concatenate([gate_grad, up_grad], axis=1).astype(jnp.bfloat16)
    output_gradient_part = adapter_scale * lax.dot_general(
        adapter_input_rows,
        joined_gradient,
        (((0,), (0,)), ((), ())),
        preferred_element_type=jnp.float32,
    )
    adapter_gradient = (
        adapter_scale
        * lax.dot_general(
            joined_gradient,
            adapter_output_weight,
            (((1,), (1,)), ((), ())),
            preferred_element_type=jnp.float32,
        )
    ).astype(jnp.bfloat16)
    grad_a = lax.dot_general(
        input_rows, adapter_gradient, (((0,), (0,)), ((), ())), preferred_element_type=jnp.float32
    )
    return (partial_value, grad_a, output_gradient_part)


def local(
    tokens,
    expert_choice_index,
    router_gate_weight,
    cotangent,
    gate_up_matrix,
    down_weight,
    adapter_input_projection,
    adapter_output_projection,
):
    devices = lax.axis_size("ea")
    experts = devices // EXPERT_SPLIT
    tok_rows, model_width = tokens.shape
    top_count = expert_choice_index.shape[1]
    capacity = 9 * tok_rows * top_count // (8 * experts)
    half_width = model_width // 2
    parity = lax.axis_index("ea") % 2
    slot_rank = slot_ranks(expert_choice_index, experts)
    slot_rows = (expert_choice_index * capacity + slot_rank).reshape(-1)
    scaled_dy = (router_gate_weight[:, :, None] * cotangent[:, None, :].astype(jnp.float32)).astype(
        jnp.bfloat16
    )
    repeated = jnp.broadcast_to(tokens[:, None, :], (tok_rows, top_count, model_width))
    both_rows = jnp.stack([repeated, scaled_dy], axis=2).reshape(
        tok_rows * top_count, 2, model_width
    )
    blank_rows = jnp.zeros((experts * capacity, 2, model_width), jnp.bfloat16)
    send_rows = blank_rows.at[slot_rows].set(both_rows, unique_indices=True)
    rows_total = devices * capacity
    halves = (
        send_rows.reshape(experts, capacity, 2, 2, half_width)
        .transpose(0, 3, 1, 2, 4)
        .reshape(devices, capacity, 2, half_width)
    )
    own_piece = lax.all_to_all(halves, "ea", split_axis=0, concat_axis=0, tiled=True)
    other_piece = from_partner(own_piece, "ea", 0)
    lower_block_part = jnp.where(parity == 0, own_piece, other_piece)
    upper_block_part = jnp.where(parity == 0, other_piece, own_piece)
    arrived = jnp.concatenate([lower_block_part, upper_block_part], axis=3)
    input_rows = arrived[:, :, 0].reshape(rows_total, model_width)
    output_gradient_rows = arrived[:, :, 1].reshape(rows_total, model_width)
    partial_value, input_gradient_local, output_gradient_part = block_halfway(
        input_rows,
        output_gradient_rows,
        gate_up_matrix[0],
        down_weight[0],
        adapter_input_projection,
        adapter_output_projection[0],
    )
    adapter_input_gradient = lax.psum(input_gradient_local, "ea")
    partial_value = partial_value.reshape(devices, capacity, model_width)
    kept_part = jnp.where(
        parity == 0, partial_value[:, :, :half_width], partial_value[:, :, half_width:]
    )
    given_part = jnp.where(
        parity == 0, partial_value[:, :, half_width:], partial_value[:, :, :half_width]
    )
    taken_part = from_partner(given_part, "ea", 0)
    summed = (kept_part.astype(jnp.float32) + taken_part.astype(jnp.float32)).astype(jnp.bfloat16)
    returned = lax.all_to_all(summed, "ea", split_axis=0, concat_axis=0, tiled=True)
    expert_out = (
        returned.reshape(experts, 2, capacity, half_width)
        .transpose(0, 2, 1, 3)
        .reshape(experts * capacity, model_width)
    )
    picked = expert_out[slot_rows].reshape(tok_rows, top_count, model_width).astype(jnp.float32)
    layer_output = jnp.sum(router_gate_weight[:, :, None] * picked, axis=1).astype(jnp.bfloat16)
    return (layer_output, adapter_input_gradient, output_gradient_part[None])


def line_local(
    tokens,
    expert_choice_index,
    router_gate_weight,
    cotangent,
    gate_up_matrix,
    down_weight,
    adapter_input_projection,
    adapter_output_projection,
):
    devices = lax.axis_size("ea")
    experts = devices // EXPERT_SPLIT
    planes = devices // PLANE
    tok_rows, model_width = tokens.shape
    top_count = expert_choice_index.shape[1]
    capacity = 9 * tok_rows * top_count // (8 * experts)
    here = lax.axis_index("ea")
    plane = here // PLANE
    mine = here // EXPERT_SPLIT
    block_width = down_weight.shape[1]
    adapter_a = adapter_input_projection
    gate_up_weight, down_w, adapter_out = gate_up_matrix[0], down_weight[0], adapter_output_projection[0]

    def up(value, low, high):
        moves = [(p * PLANE + j, (p + 1) * PLANE + j) for p in range(low, high) for j in range(PLANE)]
        return lax.ppermute(value, "ea", moves)

    def down(value, low, high):
        moves = [(p * PLANE + j, (p - 1) * PLANE + j) for p in range(low, high) for j in range(PLANE)]
        return lax.ppermute(value, "ea", moves)

    def across(value, low=0, high=planes):
        moves = [(p * PLANE + j, p * PLANE + (j ^ 2)) for p in range(low, high) for j in range(PLANE)]
        return lax.ppermute(value, "ea", moves)

    def core(value):
        return from_partner(value, "ea", 0)

    def along(value):
        rising, falling = [value], [value]
        for k in range(1, planes):
            rising.append(up(rising[-1], k - 1, planes - 1))
            falling.append(down(falling[-1], 1, planes - k + 1))
        return rising, falling

    def pick_of(info):
        named = info[None, :top_count] == jnp.stack([mine, mine ^ 1]).astype(jnp.float32)[:, None, None]
        weight = jnp.sum(jnp.where(named, info[None, top_count:], 0.0), axis=1)
        chosen = jnp.any(named, axis=1)
        place = jnp.cumsum(chosen.astype(jnp.int32), axis=1) - 1
        place = jnp.where(chosen, place, capacity)
        pick = place[:, None, :] == jnp.arange(capacity, dtype=jnp.int32)[None, :, None]
        row_weight = jnp.sum(jnp.where(pick, weight[:, None, :], 0.0), axis=2)
        return pick.astype(jnp.bfloat16), weight, row_weight

    def merge(rising, falling):
        return [rising[0]] + [
            jnp.where(plane >= d, rising[d], falling[planes - d]) for d in range(1, planes)
        ]

    def gather_rows(value, picks_up, picks_down, scaled):
        rising, falling = along(value)

        def split(block, picks, low, high):
            select, _, row_weight = picks
            rows = jnp.dot(
                select.reshape(2 * capacity, tok_rows), block, preferred_element_type=jnp.float32
            ).reshape(2, capacity, model_width)
            if scaled:
                rows = rows * row_weight[:, :, None]
            rows = rows.astype(jnp.bfloat16)
            return rows[0], across(rows[1], low, high)

        ups = [split(b, q, k, planes) for k, (b, q) in enumerate(zip(rising, picks_up))]
        downs = [ups[0]] + [
            split(falling[k], picks_down[k], 0, planes - k) for k in range(1, planes)
        ]
        own = merge([u[0] for u in ups], [d[0] for d in downs])
        other = merge([u[1] for u in ups], [d[1] for d in downs])
        lane = jnp.concatenate(own + other, axis=0)
        return jnp.concatenate([lane, core(lane)], axis=0)

    info = jnp.concatenate([expert_choice_index.T.astype(jnp.float32), router_gate_weight.T], axis=0)
    info_up, info_down = along(info)
    picks_up = [pick_of(v) for v in info_up]
    picks_down = [picks_up[0]] + [pick_of(v) for v in info_down[1:]]
    input_rows = gather_rows(tokens, picks_up, picks_down, False)
    gradient_rows = gather_rows(cotangent, picks_up, picks_down, True)

    adapter_rows = jnp.dot(input_rows, adapter_a, preferred_element_type=jnp.float32).astype(jnp.bfloat16)
    joined = jnp.dot(
        input_rows, gate_up_weight, preferred_element_type=jnp.float32
    ) + adapter_scale * jnp.dot(adapter_rows, adapter_out, preferred_element_type=jnp.float32)
    gate_part, up_part = joined[:, :block_width], joined[:, block_width:]
    sigmoid_gate = jax.nn.sigmoid(gate_part)
    active = gate_part * sigmoid_gate
    hidden = (active * up_part).astype(jnp.bfloat16)
    partial_value = jnp.dot(hidden, down_w, preferred_element_type=jnp.float32).astype(jnp.bfloat16)

    half = partial_value.shape[0] // 2
    quarter = half // 2
    taken = core(partial_value[half:])
    merged = (partial_value[:half].astype(jnp.float32) + taken.astype(jnp.float32)).astype(jnp.bfloat16)
    terms = {}
    for d in [1, planes - 1] + list(range(2, planes - 1)) + [0]:
        at = d * capacity
        foreign = across(merged[quarter + at : quarter + at + capacity])
        both = (merged[at : at + capacity], foreign)
        term = 0.0
        for i in range(2):
            if d == 0:
                select, weight = picks_up[0][0][i], picks_up[0][1][i]
            else:
                first, second = picks_up[d], picks_down[planes - d]
                select = jnp.where(plane >= d, first[0][i], second[0][i])
                weight = jnp.where(plane >= d, first[1][i], second[1][i])
            spread = lax.dot_general(
                select, both[i], (((0,), (0,)), ((), ())), preferred_element_type=jnp.float32
            )
            term = term + weight[:, None] * spread
        terms[d] = term
    rise = fall = 0.0
    for k in range(planes - 1, 0, -1):
        rise = up((terms[planes - k] + rise).astype(jnp.bfloat16), 0, planes - k).astype(jnp.float32)
        fall = down((terms[k] + fall).astype(jnp.bfloat16), k, planes).astype(jnp.float32)
    layer_output = (terms[0] + rise + fall).astype(jnp.bfloat16)

    down_grad = lax.dot_general(
        gradient_rows, down_w, (((1,), (1,)), ((), ())), preferred_element_type=jnp.float32
    )
    gate_grad = down_grad * up_part * sigmoid_gate * (1.0 + gate_part * (1.0 - sigmoid_gate))
    up_grad = down_grad * active
    joined_gradient = jnp.concatenate([gate_grad, up_grad], axis=1).astype(jnp.bfloat16)
    lora_b = adapter_scale * lax.dot_general(
        adapter_rows, joined_gradient, (((0,), (0,)), ((), ())), preferred_element_type=jnp.float32
    )
    adapter_gradient = (
        adapter_scale
        * lax.dot_general(
            joined_gradient, adapter_out, (((1,), (1,)), ((), ())), preferred_element_type=jnp.float32
        )
    ).astype(jnp.bfloat16)
    grad_a = lax.dot_general(
        adapter_gradient, input_rows, (((0,), (0,)), ((), ())), preferred_element_type=jnp.float32
    )
    distance = 0
    while 2**distance < devices:
        grad_a = grad_a + from_partner(grad_a, "ea", distance)
        distance += 1
    return (layer_output, grad_a.T, lora_b[None])


def solution(mesh):
    in_specs = (
        P(("ga", "ea"), None),
        P(("ga", "ea"), None),
        P(("ga", "ea"), None),
        P(("ga", "ea"), None),
        P("ea", None, None),
        P("ea", None, None),
        P(),
        P("ea", None, None),
    )
    out_specs = (P(("ga", "ea"), None), P("ga", None), P(("ga", "ea"), None, None))
    devices = mesh.shape["ea"]
    square = devices >= 2 * PLANE and devices & (devices - 1) == 0

    def chosen(*args):
        few = devices // EXPERT_SPLIT <= 2 * args[1].shape[1]
        body = line_local if few and square else local
        return jax.shard_map(
            body, mesh=mesh, in_specs=in_specs, out_specs=out_specs, check_vma=False
        )(*args)

    return chosen
```

```python
import functools

import jax
import jax.numpy as jnp
from jax import lax
from jax.experimental import pallas as pl
from jax.experimental.pallas import tpu as pltpu
from jax.sharding import PartitionSpec as P

EXPERT_SPLIT = 2
PLANE = 4


adapter_scale = 2.0


def from_partner(value, axis, distance):
    mask = 2**distance
    pairs = [(source, source ^ mask) for source in range(lax.axis_size(axis))]
    return lax.ppermute(value, axis, pairs)


def slot_ranks(id_block, experts):
    flat_ids = id_block.reshape(-1)
    onehot = (flat_ids[:, None] == jnp.arange(experts, dtype=jnp.int32)[None, :]).astype(jnp.int32)
    before = jnp.cumsum(onehot, axis=0) - onehot
    return jnp.sum(before * onehot, axis=1).reshape(id_block.shape)


def block_halfway(
    input_rows, output_gradient_rows, gate_up_weight, down_w, adapter_a, adapter_output_weight
):
    adapter_input_rows = jnp.dot(input_rows, adapter_a, preferred_element_type=jnp.float32).astype(
        jnp.bfloat16
    )
    joined_columns = jnp.dot(
        input_rows, gate_up_weight, preferred_element_type=jnp.float32
    ) + adapter_scale * jnp.dot(
        adapter_input_rows, adapter_output_weight, preferred_element_type=jnp.float32
    )
    block_width = down_w.shape[0]
    gate_part = joined_columns[:, :block_width]
    up_part = joined_columns[:, block_width:]
    sigmoid_gate = jax.nn.sigmoid(gate_part)
    active = gate_part * sigmoid_gate
    hidden = (active * up_part).astype(jnp.bfloat16)
    partial_value = jnp.dot(hidden, down_w, preferred_element_type=jnp.float32).astype(jnp.bfloat16)
    down_grad = lax.dot_general(
        output_gradient_rows, down_w, (((1,), (1,)), ((), ())), preferred_element_type=jnp.float32
    )
    gate_grad = down_grad * up_part * sigmoid_gate * (1.0 + gate_part * (1.0 - sigmoid_gate))
    up_grad = down_grad * active
    joined_gradient = jnp.concatenate([gate_grad, up_grad], axis=1).astype(jnp.bfloat16)
    output_gradient_part = adapter_scale * lax.dot_general(
        adapter_input_rows,
        joined_gradient,
        (((0,), (0,)), ((), ())),
        preferred_element_type=jnp.float32,
    )
    adapter_gradient = (
        adapter_scale
        * lax.dot_general(
            joined_gradient,
            adapter_output_weight,
            (((1,), (1,)), ((), ())),
            preferred_element_type=jnp.float32,
        )
    ).astype(jnp.bfloat16)
    grad_a = lax.dot_general(
        input_rows, adapter_gradient, (((0,), (0,)), ((), ())), preferred_element_type=jnp.float32
    )
    return (partial_value, grad_a, output_gradient_part)


def local(
    tokens,
    expert_choice_index,
    router_gate_weight,
    cotangent,
    gate_up_matrix,
    down_weight,
    adapter_input_projection,
    adapter_output_projection,
):
    devices = lax.axis_size("ea")
    experts = devices // EXPERT_SPLIT
    tok_rows, model_width = tokens.shape
    top_count = expert_choice_index.shape[1]
    capacity = 9 * tok_rows * top_count // (8 * experts)
    half_width = model_width // 2
    parity = lax.axis_index("ea") % 2
    slot_rank = slot_ranks(expert_choice_index, experts)
    slot_rows = (expert_choice_index * capacity + slot_rank).reshape(-1)
    scaled_dy = (router_gate_weight[:, :, None] * cotangent[:, None, :].astype(jnp.float32)).astype(
        jnp.bfloat16
    )
    repeated = jnp.broadcast_to(tokens[:, None, :], (tok_rows, top_count, model_width))
    both_rows = jnp.stack([repeated, scaled_dy], axis=2).reshape(
        tok_rows * top_count, 2, model_width
    )
    blank_rows = jnp.zeros((experts * capacity, 2, model_width), jnp.bfloat16)
    send_rows = blank_rows.at[slot_rows].set(both_rows, unique_indices=True)
    rows_total = devices * capacity
    halves = (
        send_rows.reshape(experts, capacity, 2, 2, half_width)
        .transpose(0, 3, 1, 2, 4)
        .reshape(devices, capacity, 2, half_width)
    )
    own_piece = lax.all_to_all(halves, "ea", split_axis=0, concat_axis=0, tiled=True)
    other_piece = from_partner(own_piece, "ea", 0)
    lower_block_part = jnp.where(parity == 0, own_piece, other_piece)
    upper_block_part = jnp.where(parity == 0, other_piece, own_piece)
    arrived = jnp.concatenate([lower_block_part, upper_block_part], axis=3)
    input_rows = arrived[:, :, 0].reshape(rows_total, model_width)
    output_gradient_rows = arrived[:, :, 1].reshape(rows_total, model_width)
    partial_value, input_gradient_local, output_gradient_part = block_halfway(
        input_rows,
        output_gradient_rows,
        gate_up_matrix[0],
        down_weight[0],
        adapter_input_projection,
        adapter_output_projection[0],
    )
    adapter_input_gradient = lax.psum(input_gradient_local, "ea")
    partial_value = partial_value.reshape(devices, capacity, model_width)
    kept_part = jnp.where(
        parity == 0, partial_value[:, :, :half_width], partial_value[:, :, half_width:]
    )
    given_part = jnp.where(
        parity == 0, partial_value[:, :, half_width:], partial_value[:, :, :half_width]
    )
    taken_part = from_partner(given_part, "ea", 0)
    summed = (kept_part.astype(jnp.float32) + taken_part.astype(jnp.float32)).astype(jnp.bfloat16)
    returned = lax.all_to_all(summed, "ea", split_axis=0, concat_axis=0, tiled=True)
    expert_out = (
        returned.reshape(experts, 2, capacity, half_width)
        .transpose(0, 2, 1, 3)
        .reshape(experts * capacity, model_width)
    )
    picked = expert_out[slot_rows].reshape(tok_rows, top_count, model_width).astype(jnp.float32)
    layer_output = jnp.sum(router_gate_weight[:, :, None] * picked, axis=1).astype(jnp.bfloat16)
    return (layer_output, adapter_input_gradient, output_gradient_part[None])


def picks_of(info, expert, top_count, capacity):
    tok_rows = info.shape[1]
    named = info[:top_count] == expert.astype(jnp.float32)
    weight = jnp.sum(jnp.where(named, info[top_count:], 0.0), axis=0, keepdims=True)
    chosen = jnp.sum(jnp.where(named, 1.0, 0.0), axis=0, keepdims=True)
    before = lax.broadcasted_iota(jnp.int32, (tok_rows, tok_rows), 0)
    after = lax.broadcasted_iota(jnp.int32, (tok_rows, tok_rows), 1)
    ahead = jnp.where(before < after, 1.0, 0.0).astype(jnp.bfloat16)
    place = jnp.dot(
        jnp.broadcast_to(chosen, (8, tok_rows)).astype(jnp.bfloat16),
        ahead,
        preferred_element_type=jnp.float32,
    )[:1]
    place = jnp.where(chosen > 0.0, place, -1.0)
    slots = lax.broadcasted_iota(jnp.int32, (capacity, tok_rows), 0).astype(jnp.float32)
    pick = jnp.broadcast_to(place, (capacity, tok_rows)) == slots
    return pick, weight


def remote(source, target, send_sem, recv_sem, device):
    return pltpu.make_async_remote_copy(
        src_ref=source,
        dst_ref=target,
        send_sem=send_sem,
        recv_sem=recv_sem,
        device_id={"ea": device},
        device_id_type=pl.DeviceIdType.MESH,
    )


def greet(here, plane, planes):
    barrier = pltpu.get_barrier_semaphore()

    def tell(device):
        pl.semaphore_signal(
            barrier, inc=1, device_id={"ea": device}, device_id_type=pl.DeviceIdType.MESH
        )

    tell(here + 1 - 2 * (here % 2))
    tell(here + 2 - 4 * ((here // 2) % 2))

    @pl.when(plane > 0)
    def _():
        tell(here - PLANE)

    @pl.when(plane < planes - 1)
    def _():
        tell(here + PLANE)

    ends = jnp.where(plane > 0, 1, 0) + jnp.where(plane < planes - 1, 1, 0)
    pl.semaphore_wait(barrier, 2 + ends)


def gather_kernel(
    planes, top_count, capacity,
    x_ref, c_ref, info_ref,
    rows_ref, grad_ref, infos_ref,
    line, infos, staged, load_sem, line_send, line_recv, info_send, info_recv, x_send, x_recv,
    core_send, core_recv,
):
    here = lax.axis_index("ea")
    plane = here // PLANE
    mine = here // EXPERT_SPLIT
    partner = here + 1 - 2 * (here % 2)
    beside = here + 2 - 4 * ((here // 2) % 2)
    theirs = beside // EXPERT_SPLIT
    outs = (rows_ref, grad_ref)
    loads = [
        pltpu.make_async_copy(ref, line.at[t, plane], load_sem.at[t])
        for t, ref in enumerate((x_ref, c_ref))
    ]
    for load in loads:
        load.start()
    infos[plane] = info_ref[...]
    greet(here, plane, planes)
    steps = (PLANE, -PLANE)
    can = (plane < planes - 1, plane > 0)

    def info_copy(at, way):
        return remote(
            infos.at[at], infos.at[at], info_send.at[way, at], info_recv.at[at], here + steps[way]
        )

    def line_copy(t, at, way):
        return remote(
            line.at[t, at], line.at[t, at], line_send.at[t, way, at], line_recv.at[t, at],
            here + steps[way],
        )

    def x_copy(t, at):
        return remote(
            staged.at[t, at], outs[t].at[planes + at], x_send.at[t, at], x_recv.at[t, at], beside
        )

    def core_copy(t, slot):
        return remote(
            outs[t].at[slot], outs[t].at[2 * planes + slot], core_send.at[t, slot],
            core_recv.at[t, slot], partner,
        )

    def begin(make, way):
        @pl.when(can[way])
        def _():
            make().start()

    def handle(at, ways, own):
        if not own:
            info_copy(at, 0).wait_recv()
        for way in ways:
            begin(lambda: info_copy(at, way), way)
        info = infos[at]
        ours, our_weight = picks_of(info, mine, top_count, capacity)
        others, other_weight = picks_of(info, theirs, top_count, capacity)
        select = jnp.concatenate(
            [jnp.where(ours, 1.0, 0.0), jnp.where(others, 1.0, 0.0)], axis=0
        ).astype(jnp.bfloat16)
        row_weight = jnp.concatenate(
            [
                jnp.sum(jnp.where(ours, our_weight, 0.0), axis=1, keepdims=True),
                jnp.sum(jnp.where(others, other_weight, 0.0), axis=1, keepdims=True),
            ],
            axis=0,
        )
        for t in range(2):
            if own:
                loads[t].wait()
            else:
                line_copy(t, at, 0).wait_recv()
            for way in ways:
                begin(lambda: line_copy(t, at, way), way)
            picked = jnp.dot(select, line[t, at], preferred_element_type=jnp.float32)
            if t == 1:
                picked = picked * row_weight
            picked = picked.astype(jnp.bfloat16)
            staged[t, at] = picked[capacity:]
            x_copy(t, at).start()
            outs[t][at] = picked[:capacity]
            core_copy(t, at).start()

    def relay(at):
        for t in range(2):
            x_copy(t, at).wait_recv()
            core_copy(t, planes + at).start()

    handle(plane, (0, 1), True)
    for d in range(1, planes):
        @pl.when(plane >= d)
        def _():
            handle(plane - d, (0,), False)

        @pl.when(plane + d < planes)
        def _():
            handle(plane + d, (1,), False)

        if d == 1:
            relay(plane)
        else:
            @pl.when(plane >= d - 1)
            def _():
                relay(plane - (d - 1))

            @pl.when(plane + d - 1 < planes)
            def _():
                relay(plane + (d - 1))

    @pl.when(plane >= planes - 1)
    def _():
        relay(plane - (planes - 1))

    @pl.when(plane + planes - 1 < planes)
    def _():
        relay(plane + (planes - 1))

    for at in range(planes):
        @pl.when((plane >= at) & can[0])
        def _():
            info_copy(at, 0).wait_send()
            for t in range(2):
                line_copy(t, at, 0).wait_send()

        @pl.when((plane <= at) & can[1])
        def _():
            info_copy(at, 1).wait_send()
            for t in range(2):
                line_copy(t, at, 1).wait_send()

        for t in range(2):
            x_copy(t, at).wait_send()
    for t in range(2):
        for slot in range(2 * planes):
            core_copy(t, slot).wait()
    infos_ref[...] = infos[...]


def return_kernel(
    planes, top_count, capacity,
    part_ref, infos_ref,
    out_ref,
    taken, merged, foreign, rise_in, rise_out, fall_in, fall_out,
    core_send, core_recv, x_send, x_recv, line_send, line_recv,
):
    here = lax.axis_index("ea")
    plane = here // PLANE
    mine = here // EXPERT_SPLIT
    partner = here + 1 - 2 * (here % 2)
    beside = here + 2 - 4 * ((here // 2) % 2)
    theirs = beside // EXPERT_SPLIT
    rise_in[plane] = jnp.zeros_like(rise_in[plane])
    fall_in[plane] = jnp.zeros_like(fall_in[plane])
    greet(here, plane, planes)

    def core_copy(slot):
        return remote(
            part_ref.at[2 * planes + slot], taken.at[slot], core_send.at[slot], core_recv.at[slot],
            partner,
        )

    def x_copy(at):
        return remote(
            merged.at[planes + at], foreign.at[at], x_send.at[at], x_recv.at[at], beside
        )

    def line_copy(at, way):
        out, into = (rise_out, rise_in) if way == 0 else (fall_out, fall_in)
        return remote(
            out.at[at], into.at[at], line_send.at[way, at], line_recv.at[way, at],
            here + (PLANE if way == 0 else -PLANE),
        )

    def each(body):
        for d in range(planes - 1, 0, -1):
            @pl.when(plane + d < planes)
            def _():
                body(plane + d, 0)

            @pl.when(plane >= d)
            def _():
                body(plane - d, 1)

        body(plane, 2)

    def send_core(at, way):
        core_copy(planes + at).start()
        core_copy(at).start()

    def add(slot):
        core_copy(slot).wait_recv()
        merged[slot] = (
            part_ref[slot].astype(jnp.float32) + taken[slot].astype(jnp.float32)
        ).astype(jnp.bfloat16)

    def send_x(at, way):
        add(planes + at)
        x_copy(at).start()
        add(at)

    def finish(at, way):
        info = infos_ref[at]
        x_copy(at).wait_recv()
        term = 0.0
        for expert, rows in ((mine, merged), (theirs, foreign)):
            pick, weight = picks_of(info, expert, top_count, capacity)
            spread = lax.dot_general(
                jnp.where(pick, 1.0, 0.0).astype(jnp.bfloat16),
                rows[at],
                (((0,), (0,)), ((), ())),
                preferred_element_type=jnp.float32,
            )
            column = jnp.transpose(jnp.broadcast_to(weight, (8, weight.shape[1])))[:, :1]
            term = term + column * spread
        if way == 2:
            rise_out[at] = term.astype(jnp.bfloat16)
            total = term

            @pl.when(plane > 0)
            def _():
                line_copy(at, 0).wait_recv()

            @pl.when(plane < planes - 1)
            def _():
                line_copy(at, 1).wait_recv()

            risen = jnp.where(plane > 0, rise_in[at].astype(jnp.float32), 0.0)
            fallen = jnp.where(plane < planes - 1, fall_in[at].astype(jnp.float32), 0.0)
            out_ref[...] = (total + risen + fallen).astype(out_ref.dtype)
        else:
            out, into = (rise_out, rise_in) if way == 0 else (fall_out, fall_in)
            inner = plane > 0 if way == 0 else plane < planes - 1

            @pl.when(inner)
            def _():
                line_copy(at, way).wait_recv()
                out[at] = (term + into[at].astype(jnp.float32)).astype(jnp.bfloat16)

            @pl.when(jnp.logical_not(inner))
            def _():
                out[at] = term.astype(jnp.bfloat16)

            line_copy(at, way).start()

    each(send_core)
    each(send_x)
    each(finish)
    for at in range(planes):
        x_copy(at).wait_send()

        @pl.when(plane < at)
        def _():
            line_copy(at, 0).wait_send()

        @pl.when(plane > at)
        def _():
            line_copy(at, 1).wait_send()

    for slot in range(2 * planes):
        core_copy(slot).wait_send()


def line_local(
    tokens,
    expert_choice_index,
    router_gate_weight,
    cotangent,
    gate_up_matrix,
    down_weight,
    adapter_input_projection,
    adapter_output_projection,
):
    devices = lax.axis_size("ea")
    experts = devices // EXPERT_SPLIT
    planes = devices // PLANE
    tok_rows, model_width = tokens.shape
    top_count = expert_choice_index.shape[1]
    capacity = 9 * tok_rows * top_count // (8 * experts)
    capacity = -(-capacity // 16) * 16
    block_width = down_weight.shape[1]
    adapter_a = adapter_input_projection
    gate_up_weight, down_w, adapter_out = gate_up_matrix[0], down_weight[0], adapter_output_projection[0]
    info = jnp.concatenate([expert_choice_index.T.astype(jnp.float32), router_gate_weight.T], axis=0)
    vmem = pl.BlockSpec(memory_space=pltpu.VMEM)
    anyspace = pl.BlockSpec(memory_space=pl.ANY)
    dma = pltpu.SemaphoreType.DMA
    rows_type = jax.ShapeDtypeStruct((4 * planes, capacity, model_width), jnp.bfloat16)
    input_rows, gradient_rows, infos = pl.pallas_call(
        functools.partial(gather_kernel, planes, top_count, capacity),
        out_shape=(
            rows_type, rows_type, jax.ShapeDtypeStruct((planes,) + info.shape, jnp.float32)
        ),
        in_specs=[anyspace, anyspace, vmem],
        out_specs=(vmem, vmem, vmem),
        scratch_shapes=[
            pltpu.VMEM((2, planes, tok_rows, model_width), jnp.bfloat16),
            pltpu.VMEM((planes,) + info.shape, jnp.float32),
            pltpu.VMEM((2, planes, capacity, model_width), jnp.bfloat16),
            dma((2,)), dma((2, 2, planes)), dma((2, planes)), dma((2, planes)), dma((planes,)),
            dma((2, planes)), dma((2, planes)), dma((2, 2 * planes)), dma((2, 2 * planes)),
        ],
        compiler_params=pltpu.CompilerParams(
            collective_id=0, has_side_effects=True, vmem_limit_bytes=40 * 2**20
        ),
        name="gather_rows",
    )(tokens, cotangent, info)
    input_rows = input_rows.reshape(-1, model_width)
    gradient_rows = gradient_rows.reshape(-1, model_width)

    adapter_rows = jnp.dot(input_rows, adapter_a, preferred_element_type=jnp.float32).astype(jnp.bfloat16)
    joined = jnp.dot(
        input_rows, gate_up_weight, preferred_element_type=jnp.float32
    ) + adapter_scale * jnp.dot(adapter_rows, adapter_out, preferred_element_type=jnp.float32)
    gate_part, up_part = joined[:, :block_width], joined[:, block_width:]
    sigmoid_gate = jax.nn.sigmoid(gate_part)
    active = gate_part * sigmoid_gate
    hidden = (active * up_part).astype(jnp.bfloat16)
    partial_value = jnp.dot(hidden, down_w, preferred_element_type=jnp.float32).astype(jnp.bfloat16)

    down_grad = lax.dot_general(
        gradient_rows, down_w, (((1,), (1,)), ((), ())), preferred_element_type=jnp.float32
    )
    gate_grad = down_grad * up_part * sigmoid_gate * (1.0 + gate_part * (1.0 - sigmoid_gate))
    up_grad = down_grad * active
    joined_gradient = jnp.concatenate([gate_grad, up_grad], axis=1).astype(jnp.bfloat16)
    lora_b = adapter_scale * lax.dot_general(
        adapter_rows, joined_gradient, (((0,), (0,)), ((), ())), preferred_element_type=jnp.float32
    )
    adapter_gradient = (
        adapter_scale
        * lax.dot_general(
            joined_gradient, adapter_out, (((1,), (1,)), ((), ())), preferred_element_type=jnp.float32
        )
    ).astype(jnp.bfloat16)
    grad_a = lax.dot_general(
        adapter_gradient, input_rows, (((0,), (0,)), ((), ())), preferred_element_type=jnp.float32
    )
    block = (tok_rows, model_width)
    layer_output = pl.pallas_call(
        functools.partial(return_kernel, planes, top_count, capacity),
        out_shape=jax.ShapeDtypeStruct(block, jnp.bfloat16),
        in_specs=[vmem, vmem],
        out_specs=vmem,
        scratch_shapes=[
            pltpu.VMEM((2 * planes, capacity, model_width), jnp.bfloat16),
            pltpu.VMEM((2 * planes, capacity, model_width), jnp.bfloat16),
            pltpu.VMEM((planes, capacity, model_width), jnp.bfloat16),
        ]
        + [pltpu.VMEM((planes,) + block, jnp.bfloat16)] * 4
        + [
            dma((2 * planes,)), dma((2 * planes,)), dma((planes,)), dma((planes,)),
            dma((2, planes)), dma((2, planes)),
        ],
        compiler_params=pltpu.CompilerParams(
            collective_id=1, has_side_effects=True, vmem_limit_bytes=40 * 2**20
        ),
        name="return_rows",
    )(partial_value.reshape(4 * planes, capacity, model_width), infos)
    distance = 0
    while 2**distance < devices:
        grad_a = grad_a + from_partner(grad_a, "ea", distance)
        distance += 1
    return (layer_output, grad_a.T, lora_b[None])


def solution(mesh):
    in_specs = (
        P(("ga", "ea"), None),
        P(("ga", "ea"), None),
        P(("ga", "ea"), None),
        P(("ga", "ea"), None),
        P("ea", None, None),
        P("ea", None, None),
        P(),
        P("ea", None, None),
    )
    out_specs = (P(("ga", "ea"), None), P("ga", None), P(("ga", "ea"), None, None))
    devices = mesh.shape["ea"]
    square = devices >= 2 * PLANE and devices & (devices - 1) == 0

    def chosen(*args):
        few = devices // EXPERT_SPLIT <= 2 * args[1].shape[1]
        body = line_local if few and square else local
        return jax.shard_map(
            body, mesh=mesh, in_specs=in_specs, out_specs=out_specs, check_vma=False
        )(*args)

    return chosen
```

```python
import functools

import jax
import jax.numpy as jnp
from jax import lax
from jax.experimental import pallas as pl
from jax.experimental.pallas import tpu as pltpu
from jax.sharding import PartitionSpec as P

EXPERT_SPLIT = 2
PLANE = 4


adapter_scale = 2.0


def from_partner(value, axis, distance):
    mask = 2**distance
    pairs = [(source, source ^ mask) for source in range(lax.axis_size(axis))]
    return lax.ppermute(value, axis, pairs)


def slot_ranks(id_block, experts):
    flat_ids = id_block.reshape(-1)
    onehot = (flat_ids[:, None] == jnp.arange(experts, dtype=jnp.int32)[None, :]).astype(jnp.int32)
    before = jnp.cumsum(onehot, axis=0) - onehot
    return jnp.sum(before * onehot, axis=1).reshape(id_block.shape)


def block_halfway(
    input_rows, output_gradient_rows, gate_up_weight, down_w, adapter_a, adapter_output_weight
):
    adapter_input_rows = jnp.dot(input_rows, adapter_a, preferred_element_type=jnp.float32).astype(
        jnp.bfloat16
    )
    joined_columns = jnp.dot(
        input_rows, gate_up_weight, preferred_element_type=jnp.float32
    ) + adapter_scale * jnp.dot(
        adapter_input_rows, adapter_output_weight, preferred_element_type=jnp.float32
    )
    block_width = down_w.shape[0]
    gate_part = joined_columns[:, :block_width]
    up_part = joined_columns[:, block_width:]
    sigmoid_gate = jax.nn.sigmoid(gate_part)
    active = gate_part * sigmoid_gate
    hidden = (active * up_part).astype(jnp.bfloat16)
    partial_value = jnp.dot(hidden, down_w, preferred_element_type=jnp.float32).astype(jnp.bfloat16)
    down_grad = lax.dot_general(
        output_gradient_rows, down_w, (((1,), (1,)), ((), ())), preferred_element_type=jnp.float32
    )
    gate_grad = down_grad * up_part * sigmoid_gate * (1.0 + gate_part * (1.0 - sigmoid_gate))
    up_grad = down_grad * active
    joined_gradient = jnp.concatenate([gate_grad, up_grad], axis=1).astype(jnp.bfloat16)
    output_gradient_part = adapter_scale * lax.dot_general(
        adapter_input_rows,
        joined_gradient,
        (((0,), (0,)), ((), ())),
        preferred_element_type=jnp.float32,
    )
    adapter_gradient = (
        adapter_scale
        * lax.dot_general(
            joined_gradient,
            adapter_output_weight,
            (((1,), (1,)), ((), ())),
            preferred_element_type=jnp.float32,
        )
    ).astype(jnp.bfloat16)
    grad_a = lax.dot_general(
        input_rows, adapter_gradient, (((0,), (0,)), ((), ())), preferred_element_type=jnp.float32
    )
    return (partial_value, grad_a, output_gradient_part)


def local(
    tokens,
    expert_choice_index,
    router_gate_weight,
    cotangent,
    gate_up_matrix,
    down_weight,
    adapter_input_projection,
    adapter_output_projection,
):
    devices = lax.axis_size("ea")
    experts = devices // EXPERT_SPLIT
    tok_rows, model_width = tokens.shape
    top_count = expert_choice_index.shape[1]
    capacity = 9 * tok_rows * top_count // (8 * experts)
    half_width = model_width // 2
    parity = lax.axis_index("ea") % 2
    slot_rank = slot_ranks(expert_choice_index, experts)
    slot_rows = (expert_choice_index * capacity + slot_rank).reshape(-1)
    scaled_dy = (router_gate_weight[:, :, None] * cotangent[:, None, :].astype(jnp.float32)).astype(
        jnp.bfloat16
    )
    repeated = jnp.broadcast_to(tokens[:, None, :], (tok_rows, top_count, model_width))
    both_rows = jnp.stack([repeated, scaled_dy], axis=2).reshape(
        tok_rows * top_count, 2, model_width
    )
    blank_rows = jnp.zeros((experts * capacity, 2, model_width), jnp.bfloat16)
    send_rows = blank_rows.at[slot_rows].set(both_rows, unique_indices=True)
    rows_total = devices * capacity
    halves = (
        send_rows.reshape(experts, capacity, 2, 2, half_width)
        .transpose(0, 3, 1, 2, 4)
        .reshape(devices, capacity, 2, half_width)
    )
    own_piece = lax.all_to_all(halves, "ea", split_axis=0, concat_axis=0, tiled=True)
    other_piece = from_partner(own_piece, "ea", 0)
    lower_block_part = jnp.where(parity == 0, own_piece, other_piece)
    upper_block_part = jnp.where(parity == 0, other_piece, own_piece)
    arrived = jnp.concatenate([lower_block_part, upper_block_part], axis=3)
    input_rows = arrived[:, :, 0].reshape(rows_total, model_width)
    output_gradient_rows = arrived[:, :, 1].reshape(rows_total, model_width)
    partial_value, input_gradient_local, output_gradient_part = block_halfway(
        input_rows,
        output_gradient_rows,
        gate_up_matrix[0],
        down_weight[0],
        adapter_input_projection,
        adapter_output_projection[0],
    )
    adapter_input_gradient = lax.psum(input_gradient_local, "ea")
    partial_value = partial_value.reshape(devices, capacity, model_width)
    kept_part = jnp.where(
        parity == 0, partial_value[:, :, :half_width], partial_value[:, :, half_width:]
    )
    given_part = jnp.where(
        parity == 0, partial_value[:, :, half_width:], partial_value[:, :, :half_width]
    )
    taken_part = from_partner(given_part, "ea", 0)
    summed = (kept_part.astype(jnp.float32) + taken_part.astype(jnp.float32)).astype(jnp.bfloat16)
    returned = lax.all_to_all(summed, "ea", split_axis=0, concat_axis=0, tiled=True)
    expert_out = (
        returned.reshape(experts, 2, capacity, half_width)
        .transpose(0, 2, 1, 3)
        .reshape(experts * capacity, model_width)
    )
    picked = expert_out[slot_rows].reshape(tok_rows, top_count, model_width).astype(jnp.float32)
    layer_output = jnp.sum(router_gate_weight[:, :, None] * picked, axis=1).astype(jnp.bfloat16)
    return (layer_output, adapter_input_gradient, output_gradient_part[None])


def picks_of(info, expert, top_count, capacity):
    tok_rows = info.shape[1]
    named = info[:top_count] == expert.astype(jnp.float32)
    weight = jnp.sum(jnp.where(named, info[top_count:], 0.0), axis=0, keepdims=True)
    chosen = jnp.sum(jnp.where(named, 1.0, 0.0), axis=0, keepdims=True)
    before = lax.broadcasted_iota(jnp.int32, (tok_rows, tok_rows), 0)
    after = lax.broadcasted_iota(jnp.int32, (tok_rows, tok_rows), 1)
    ahead = jnp.where(before < after, 1.0, 0.0).astype(jnp.bfloat16)
    place = jnp.dot(
        jnp.broadcast_to(chosen, (8, tok_rows)).astype(jnp.bfloat16),
        ahead,
        preferred_element_type=jnp.float32,
    )[:1]
    place = jnp.where(chosen > 0.0, place, -1.0)
    slots = lax.broadcasted_iota(jnp.int32, (capacity, tok_rows), 0).astype(jnp.float32)
    pick = jnp.broadcast_to(place, (capacity, tok_rows)) == slots
    return pick, weight


def remote(source, target, send_sem, recv_sem, device):
    return pltpu.make_async_remote_copy(
        src_ref=source,
        dst_ref=target,
        send_sem=send_sem,
        recv_sem=recv_sem,
        device_id={"ea": device},
        device_id_type=pl.DeviceIdType.MESH,
    )


def greet(here, plane, planes, extra=()):
    barrier = pltpu.get_barrier_semaphore()

    def tell(device):
        pl.semaphore_signal(
            barrier, inc=1, device_id={"ea": device}, device_id_type=pl.DeviceIdType.MESH
        )

    tell(here + 1 - 2 * (here % 2))
    tell(here + 2 - 4 * ((here // 2) % 2))

    @pl.when(plane > 0)
    def _():
        tell(here - PLANE)

    @pl.when(plane < planes - 1)
    def _():
        tell(here + PLANE)

    for device in extra:
        tell(device)
    ends = jnp.where(plane > 0, 1, 0) + jnp.where(plane < planes - 1, 1, 0)
    pl.semaphore_wait(barrier, 2 + len(extra) + ends)


def gather_kernel(
    planes, top_count, capacity,
    x_ref, c_ref, info_ref,
    rows_ref, grad_ref, infos_ref,
    line, infos, staged, load_sem, line_send, line_recv, info_send, info_recv, x_send, x_recv,
    core_send, core_recv,
):
    here = lax.axis_index("ea")
    plane = here // PLANE
    mine = here // EXPERT_SPLIT
    partner = here + 1 - 2 * (here % 2)
    beside = here + 2 - 4 * ((here // 2) % 2)
    theirs = beside // EXPERT_SPLIT
    outs = (rows_ref, grad_ref)
    loads = [
        pltpu.make_async_copy(ref, line.at[t, plane], load_sem.at[t])
        for t, ref in enumerate((x_ref, c_ref))
    ]
    for load in loads:
        load.start()
    infos[plane] = info_ref[...]
    greet(here, plane, planes)
    steps = (PLANE, -PLANE)
    can = (plane < planes - 1, plane > 0)

    def info_copy(at, way):
        return remote(
            infos.at[at], infos.at[at], info_send.at[way, at], info_recv.at[at], here + steps[way]
        )

    def line_copy(t, at, way):
        return remote(
            line.at[t, at], line.at[t, at], line_send.at[t, way, at], line_recv.at[t, at],
            here + steps[way],
        )

    def x_copy(t, at):
        return remote(
            staged.at[t, at], outs[t].at[planes + at], x_send.at[t, at], x_recv.at[t, at], beside
        )

    def core_copy(t, slot):
        return remote(
            outs[t].at[slot], outs[t].at[2 * planes + slot], core_send.at[t, slot],
            core_recv.at[t, slot], partner,
        )

    def begin(make, way):
        @pl.when(can[way])
        def _():
            make().start()

    def handle(at, ways, own):
        if not own:
            info_copy(at, 0).wait_recv()
        for way in ways:
            begin(lambda: info_copy(at, way), way)
        info = infos[at]
        ours, our_weight = picks_of(info, mine, top_count, capacity)
        others, other_weight = picks_of(info, theirs, top_count, capacity)
        select = jnp.concatenate(
            [jnp.where(ours, 1.0, 0.0), jnp.where(others, 1.0, 0.0)], axis=0
        ).astype(jnp.bfloat16)
        row_weight = jnp.concatenate(
            [
                jnp.sum(jnp.where(ours, our_weight, 0.0), axis=1, keepdims=True),
                jnp.sum(jnp.where(others, other_weight, 0.0), axis=1, keepdims=True),
            ],
            axis=0,
        )
        for t in range(2):
            if own:
                loads[t].wait()
            else:
                line_copy(t, at, 0).wait_recv()
            for way in ways:
                begin(lambda: line_copy(t, at, way), way)
            picked = jnp.dot(select, line[t, at], preferred_element_type=jnp.float32)
            if t == 1:
                picked = picked * row_weight
            picked = picked.astype(jnp.bfloat16)
            staged[t, at] = picked[capacity:]
            x_copy(t, at).start()
            outs[t][at] = picked[:capacity]
            core_copy(t, at).start()

    def relay(at):
        for t in range(2):
            x_copy(t, at).wait_recv()
            core_copy(t, planes + at).start()

    handle(plane, (0, 1), True)
    for d in range(1, planes):
        @pl.when(plane >= d)
        def _():
            handle(plane - d, (0,), False)

        @pl.when(plane + d < planes)
        def _():
            handle(plane + d, (1,), False)

        if d == 1:
            relay(plane)
        else:
            @pl.when(plane >= d - 1)
            def _():
                relay(plane - (d - 1))

            @pl.when(plane + d - 1 < planes)
            def _():
                relay(plane + (d - 1))

    @pl.when(plane >= planes - 1)
    def _():
        relay(plane - (planes - 1))

    @pl.when(plane + planes - 1 < planes)
    def _():
        relay(plane + (planes - 1))

    for at in range(planes):
        @pl.when((plane >= at) & can[0])
        def _():
            info_copy(at, 0).wait_send()
            for t in range(2):
                line_copy(t, at, 0).wait_send()

        @pl.when((plane <= at) & can[1])
        def _():
            info_copy(at, 1).wait_send()
            for t in range(2):
                line_copy(t, at, 1).wait_send()

        for t in range(2):
            x_copy(t, at).wait_send()
    for t in range(2):
        for slot in range(2 * planes):
            core_copy(t, slot).wait()
    infos_ref[...] = infos[...]


def return_kernel(
    planes, top_count, capacity,
    part_ref, infos_ref, grad_ref,
    out_ref, total_ref,
    taken, merged, foreign, rise_in, rise_out, fall_in, fall_out, sums, sums_in,
    core_send, core_recv, x_send, x_recv, line_send, line_recv, grad_send, grad_recv,
):
    here = lax.axis_index("ea")
    plane = here // PLANE
    mine = here // EXPERT_SPLIT
    partner = here + 1 - 2 * (here % 2)
    beside = here + 2 - 4 * ((here // 2) % 2)
    theirs = beside // EXPERT_SPLIT
    sums[0] = grad_ref[...]
    stages = sums.shape[0] - 1
    mates = [here + 2**i - 2 ** (i + 1) * ((here // 2**i) % 2) for i in range(stages)]
    rise_in[plane] = jnp.zeros_like(rise_in[plane])
    fall_in[plane] = jnp.zeros_like(fall_in[plane])
    greet(here, plane, planes, mates[3:])

    def sum_copy(i):
        return remote(sums.at[i], sums_in.at[i], grad_send.at[i], grad_recv.at[i], mates[i])

    def next_sum(i):
        sum_copy(i - 1).wait_recv()
        sums[i] = sums[i - 1] + sums_in[i - 1]
        if i < stages:
            sum_copy(i).start()

    def core_copy(slot):
        return remote(
            part_ref.at[2 * planes + slot], taken.at[slot], core_send.at[slot], core_recv.at[slot],
            partner,
        )

    def x_copy(at):
        return remote(
            merged.at[planes + at], foreign.at[at], x_send.at[at], x_recv.at[at], beside
        )

    def line_copy(at, way):
        out, into = (rise_out, rise_in) if way == 0 else (fall_out, fall_in)
        return remote(
            out.at[at], into.at[at], line_send.at[way, at], line_recv.at[way, at],
            here + (PLANE if way == 0 else -PLANE),
        )

    def each(body, least=0, most=planes - 1):
        for d in range(most, max(least, 1) - 1, -1):
            @pl.when(plane + d < planes)
            def _():
                body(plane + d, 0)

            @pl.when(plane >= d)
            def _():
                body(plane - d, 1)

        if least == 0:
            body(plane, 2)

    def send_core(at, way):
        core_copy(planes + at).start()
        core_copy(at).start()

    def add(slot):
        core_copy(slot).wait_recv()
        merged[slot] = (
            part_ref[slot].astype(jnp.float32) + taken[slot].astype(jnp.float32)
        ).astype(jnp.bfloat16)

    def send_x(at, way):
        add(planes + at)
        x_copy(at).start()
        add(at)

    def finish(at, way):
        info = infos_ref[at]
        x_copy(at).wait_recv()
        term = 0.0
        for expert, rows in ((mine, merged), (theirs, foreign)):
            pick, weight = picks_of(info, expert, top_count, capacity)
            spread = lax.dot_general(
                jnp.where(pick, 1.0, 0.0).astype(jnp.bfloat16),
                rows[at],
                (((0,), (0,)), ((), ())),
                preferred_element_type=jnp.float32,
            )
            column = jnp.transpose(jnp.broadcast_to(weight, (8, weight.shape[1])))[:, :1]
            term = term + column * spread
        if way == 2:
            rise_out[at] = term.astype(jnp.bfloat16)
            total = term

            @pl.when(plane > 0)
            def _():
                line_copy(at, 0).wait_recv()

            @pl.when(plane < planes - 1)
            def _():
                line_copy(at, 1).wait_recv()

            risen = jnp.where(plane > 0, rise_in[at].astype(jnp.float32), 0.0)
            fallen = jnp.where(plane < planes - 1, fall_in[at].astype(jnp.float32), 0.0)
            out_ref[...] = (total + risen + fallen).astype(out_ref.dtype)
        else:
            out, into = (rise_out, rise_in) if way == 0 else (fall_out, fall_in)
            inner = plane > 0 if way == 0 else plane < planes - 1

            @pl.when(inner)
            def _():
                line_copy(at, way).wait_recv()
                out[at] = (term + into[at].astype(jnp.float32)).astype(jnp.bfloat16)

            @pl.when(jnp.logical_not(inner))
            def _():
                out[at] = term.astype(jnp.bfloat16)

            line_copy(at, way).start()

    sum_copy(0).start()
    each(send_core)
    next_sum(1)
    each(send_x)
    next_sum(2)
    each(finish, 2)
    for i in range(3, stages):
        next_sum(i)
    each(finish, 0, 1)
    next_sum(stages)
    total_ref[...] = sums[stages]
    for i in range(stages):
        sum_copy(i).wait_send()
    for at in range(planes):
        x_copy(at).wait_send()

        @pl.when(plane < at)
        def _():
            line_copy(at, 0).wait_send()

        @pl.when(plane > at)
        def _():
            line_copy(at, 1).wait_send()

    for slot in range(2 * planes):
        core_copy(slot).wait_send()


def line_local(
    tokens,
    expert_choice_index,
    router_gate_weight,
    cotangent,
    gate_up_matrix,
    down_weight,
    adapter_input_projection,
    adapter_output_projection,
):
    devices = lax.axis_size("ea")
    experts = devices // EXPERT_SPLIT
    planes = devices // PLANE
    tok_rows, model_width = tokens.shape
    top_count = expert_choice_index.shape[1]
    capacity = 9 * tok_rows * top_count // (8 * experts)
    capacity = -(-capacity // 16) * 16
    block_width = down_weight.shape[1]
    adapter_a = adapter_input_projection
    gate_up_weight, down_w, adapter_out = gate_up_matrix[0], down_weight[0], adapter_output_projection[0]
    info = jnp.concatenate([expert_choice_index.T.astype(jnp.float32), router_gate_weight.T], axis=0)
    vmem = pl.BlockSpec(memory_space=pltpu.VMEM)
    anyspace = pl.BlockSpec(memory_space=pl.ANY)
    dma = pltpu.SemaphoreType.DMA
    rows_type = jax.ShapeDtypeStruct((4 * planes, capacity, model_width), jnp.bfloat16)
    input_rows, gradient_rows, infos = pl.pallas_call(
        functools.partial(gather_kernel, planes, top_count, capacity),
        out_shape=(
            rows_type, rows_type, jax.ShapeDtypeStruct((planes,) + info.shape, jnp.float32)
        ),
        in_specs=[anyspace, anyspace, vmem],
        out_specs=(vmem, vmem, vmem),
        scratch_shapes=[
            pltpu.VMEM((2, planes, tok_rows, model_width), jnp.bfloat16),
            pltpu.VMEM((planes,) + info.shape, jnp.float32),
            pltpu.VMEM((2, planes, capacity, model_width), jnp.bfloat16),
            dma((2,)), dma((2, 2, planes)), dma((2, planes)), dma((2, planes)), dma((planes,)),
            dma((2, planes)), dma((2, planes)), dma((2, 2 * planes)), dma((2, 2 * planes)),
        ],
        compiler_params=pltpu.CompilerParams(
            collective_id=0, has_side_effects=True, vmem_limit_bytes=40 * 2**20
        ),
        name="gather_rows",
    )(tokens, cotangent, info)
    input_rows = input_rows.reshape(-1, model_width)
    gradient_rows = gradient_rows.reshape(-1, model_width)

    adapter_rows = jnp.dot(input_rows, adapter_a, preferred_element_type=jnp.float32).astype(jnp.bfloat16)
    joined = jnp.dot(
        input_rows, gate_up_weight, preferred_element_type=jnp.float32
    ) + adapter_scale * jnp.dot(adapter_rows, adapter_out, preferred_element_type=jnp.float32)
    gate_part, up_part = joined[:, :block_width], joined[:, block_width:]
    sigmoid_gate = jax.nn.sigmoid(gate_part)
    active = gate_part * sigmoid_gate
    hidden = (active * up_part).astype(jnp.bfloat16)
    partial_value = jnp.dot(hidden, down_w, preferred_element_type=jnp.float32).astype(jnp.bfloat16)

    down_grad = lax.dot_general(
        gradient_rows, down_w, (((1,), (1,)), ((), ())), preferred_element_type=jnp.float32
    )
    gate_grad = down_grad * up_part * sigmoid_gate * (1.0 + gate_part * (1.0 - sigmoid_gate))
    up_grad = down_grad * active
    joined_gradient = jnp.concatenate([gate_grad, up_grad], axis=1).astype(jnp.bfloat16)
    lora_b = adapter_scale * lax.dot_general(
        adapter_rows, joined_gradient, (((0,), (0,)), ((), ())), preferred_element_type=jnp.float32
    )
    adapter_gradient = (
        adapter_scale
        * lax.dot_general(
            joined_gradient, adapter_out, (((1,), (1,)), ((), ())), preferred_element_type=jnp.float32
        )
    ).astype(jnp.bfloat16)
    grad_a = lax.dot_general(
        adapter_gradient, input_rows, (((0,), (0,)), ((), ())), preferred_element_type=jnp.float32
    )
    block = (tok_rows, model_width)
    stages = devices.bit_length() - 1
    layer_output, grad_a = pl.pallas_call(
        functools.partial(return_kernel, planes, top_count, capacity),
        out_shape=(
            jax.ShapeDtypeStruct(block, jnp.bfloat16),
            jax.ShapeDtypeStruct(grad_a.shape, jnp.float32),
        ),
        in_specs=[vmem, vmem, vmem],
        out_specs=(vmem, vmem),
        scratch_shapes=[
            pltpu.VMEM((2 * planes, capacity, model_width), jnp.bfloat16),
            pltpu.VMEM((2 * planes, capacity, model_width), jnp.bfloat16),
            pltpu.VMEM((planes, capacity, model_width), jnp.bfloat16),
        ]
        + [pltpu.VMEM((planes,) + block, jnp.bfloat16)] * 4
        + [
            pltpu.VMEM((stages + 1,) + grad_a.shape, jnp.float32),
            pltpu.VMEM((stages,) + grad_a.shape, jnp.float32),
        ]
        + [
            dma((2 * planes,)), dma((2 * planes,)), dma((planes,)), dma((planes,)),
            dma((2, planes)), dma((2, planes)), dma((stages,)), dma((stages,)),
        ],
        compiler_params=pltpu.CompilerParams(
            collective_id=1, has_side_effects=True, vmem_limit_bytes=40 * 2**20
        ),
        name="return_rows",
    )(partial_value.reshape(4 * planes, capacity, model_width), infos, grad_a)
    return (layer_output, grad_a.T, lora_b[None])


def solution(mesh):
    in_specs = (
        P(("ga", "ea"), None),
        P(("ga", "ea"), None),
        P(("ga", "ea"), None),
        P(("ga", "ea"), None),
        P("ea", None, None),
        P("ea", None, None),
        P(),
        P("ea", None, None),
    )
    out_specs = (P(("ga", "ea"), None), P("ga", None), P(("ga", "ea"), None, None))
    devices = mesh.shape["ea"]
    square = devices >= 2 * PLANE and devices & (devices - 1) == 0

    def chosen(*args):
        few = devices // EXPERT_SPLIT <= 2 * args[1].shape[1]
        body = line_local if few and square else local
        return jax.shard_map(
            body, mesh=mesh, in_specs=in_specs, out_specs=out_specs, check_vma=False
        )(*args)

    return chosen
```
